256 devices in a mesh: pipe: 16 (over y_hi, z), vocab: 16 (over y_lo, x, core).
Axes of the slice: x: 4, y: 4 (y_hi: 2, y_lo: 2; y = y_hi * 2 + y_lo), z: 8, core: 2. Of those that a mesh axis runs over, the one named last changes fastest.
Arguments:
- final_hidden: bfloat16 [512, 4608], P('pipe', 'vocab'), may hold values from -6 to 6
- tied_table: bfloat16 [163840, 4608], P(('pipe', 'vocab')), may hold values from -1.2 to 1.2
- target_ids: int32 [512], replicated, may hold values from 0 to 163839
- input_ids: int32 [512], replicated, may hold values from 0 to 163839
- embed_cot: bfloat16 [512, 4608], P('pipe', 'vocab'), may hold values from -0.3125 to 0.3125
Outputs:
- grad_table: bfloat16 [163840, 4608], P(('pipe', 'vocab'))
- grad_hidden: float32 [512, 4608], P('pipe', 'vocab')
- token_loss: float32 [512], P('pipe')
The draws below stay inside these ranges and needn't reach their ends.
All inputs are finite; a program needn't handle non-finite values.
Results may differ from the reference program's by a relative error of at most 0.01.
Values may be sent and summed in bfloat16 or wider, within the bound.
A program may use at most 128 MiB of HBM per device.

```python
import math
import jax
import jax.numpy as jnp
import numpy as np

D = 4608
VOCAB = 163840
TOKENS = 512


def draw_tied_table(key, part):
    key_scale = jax.random.fold_in(key, 11)
    key_base = jax.random.fold_in(key, 23)
    key_order = jax.random.fold_in(key, 37)
    shuffled = jax.random.permutation(key_order, VOCAB)
    row_frac = shuffled.astype(jnp.float32)[:, None] / VOCAB
    row_scale = 0.012 * jnp.exp(jax.random.uniform(key_scale, (VOCAB, 1), jnp.float32, 0.0, math.log(4.0))) * (1.0 + 2.0 * row_frac)
    base_draw = jnp.clip(jax.random.normal(key_base, (VOCAB, D), jnp.float32), -5.0, 5.0)
    return (base_draw * row_scale).astype(jnp.bfloat16)


def plant(values, own_key, low, largest):
    shape = values.shape
    spot = [jax.random.randint(jax.random.fold_in(own_key, axis), (), 0, shape[axis]) for axis in range(len(shape))]
    values = values.at[tuple(spot)].set(low)
    longest = shape.index(max(shape))
    spot[longest] = (spot[longest] + 1) % shape[longest]
    return values.at[tuple(spot)].set(largest)


def block_scale(stream_key, extent, cuts, least, largest):
    factor_of = 1.0
    for position, parts in cuts:
        heights = jax.random.uniform(jax.random.fold_in(jax.random.fold_in(stream_key, 6), position), (parts,), jnp.float32, least / len(cuts), largest / len(cuts))
        factor_of = factor_of * jnp.repeat(jnp.exp(heights), extent[position] // parts).reshape((-1,) + (1,) * (len(extent) - 1 - position))
    return factor_of


def ranked_wide(stream_key, dims, amount, skew):
    loads = [min(1 << octave, amount + 1 - (1 << octave)) * (1 << 20) // math.isqrt((1 << octave) ** skew) + 1 for octave in range((amount + 1).bit_length()) if 1 << octave <= amount]
    deviation = 1 + sum(loads) // (1 << 30)
    listing = np.cumsum(np.array([max(1, weight // deviation) for weight in loads]))
    lot = jax.random.randint(jax.random.fold_in(stream_key, 1), dims, 0, int(listing[len(loads) - 1]))
    start = jnp.left_shift(1, jnp.searchsorted(jnp.asarray(listing, jnp.int32), lot, side="right").astype(jnp.int32))
    grade = start - 1 + jax.random.randint(jax.random.fold_in(stream_key, 4), dims, 0, 1 << 30) % jnp.minimum(start, amount + 1 - start)
    return jax.random.permutation(jax.random.fold_in(stream_key, 2), amount)[grade].astype(jnp.int32)


def gaussian(own_key, extent, width, limit, cuts=(), dtype=jnp.bfloat16):
    entries = width * jax.random.normal(own_key, extent, jnp.float32)
    if cuts:
        entries = entries * block_scale(own_key, extent, cuts, -0.22, 0.18)
    return jnp.clip(entries, -limit, limit).astype(dtype)


def setup_inputs(seed: int = 0) -> dict:
    streams_of = jax.random.split(jax.random.key(seed), 6)
    return {
        "final_hidden": gaussian(streams_of[0], (TOKENS, D), 1.0, 6.0, ((0, 16), (1, 16))),
        "tied_table": draw_tied_table(jax.random.fold_in(streams_of[5], 71), 0),
        "target_ids": plant(ranked_wide(streams_of[2], (TOKENS,), VOCAB, 2), jax.random.fold_in(streams_of[2], 3), 0, VOCAB - 1).astype(jnp.int32),
        "input_ids": plant(ranked_wide(streams_of[3], (TOKENS,), VOCAB, 2), jax.random.fold_in(streams_of[3], 3), 0, VOCAB - 1).astype(jnp.int32),
        "embed_cot": gaussian(streams_of[4], (TOKENS, D), 0.02, 0.3125, ((0, 16), (1, 16))),
    }


def reference(final_hidden, tied_table, target_ids, input_ids, embed_cot):
    logits = jnp.dot(final_hidden, tied_table.T, preferred_element_type=jnp.float32)
    tanh_part = jnp.tanh(logits / 30.0)
    capped = 30.0 * tanh_part
    exponent = jnp.exp(capped)
    sum_exp = jnp.sum(exponent, axis=1)
    target_mask = jnp.arange(VOCAB)[None, :] == target_ids[:, None]
    target_logit = jnp.sum(jnp.where(target_mask, capped, 0.0), axis=1)
    token_loss = jnp.log(sum_exp) - target_logit
    dlogits = ((exponent / sum_exp[:, None] - target_mask.astype(jnp.float32)) * (1.0 - tanh_part * tanh_part)).astype(jnp.bfloat16)
    grad_hidden = jnp.dot(dlogits, tied_table, preferred_element_type=jnp.float32)
    head_grad = jnp.dot(dlogits.T, final_hidden, preferred_element_type=jnp.float32)
    embed_grad = jax.ops.segment_sum(embed_cot.astype(jnp.float32), input_ids, num_segments=VOCAB)
    grad_table = (head_grad + (float(D) ** 0.5) * embed_grad).astype(jnp.bfloat16)
    return grad_table, grad_hidden, token_loss
```

```python
import jax
import jax.numpy as jnp
from jax import lax
from jax.experimental import pallas as pl
from jax.experimental.pallas import tpu as pltpu
from jax.sharding import PartitionSpec as P

D = 4608
HALF = D // 2
ROWS = 640
TOKENS = 512
PIECE = 288
BF = jnp.bfloat16
F32 = jnp.float32
MESH = pl.DeviceIdType.MESH
NT = (((1,), (1,)), ((), ()))


def rcopy(src, dst, send, recv, p, v):
    return pltpu.make_async_remote_copy(
        src_ref=src, dst_ref=dst, send_sem=send, recv_sem=recv, device_id=(p, v), device_id_type=MESH
    )


def kernel(
    h_in, w_hbm, tgt_ref, ids_ref, c_in,
    grad_out, hid_out, loss_out,
    w, h_buf, c_buf, tanh_buf, dl, dlt, pair, rbuf, g_buf,
    s1, ar_src, ar_v, ar_p, y_buf, v_src, v_buf,
    w_sem, s1s, s1r, ys, yr, zs, zr, cs, cr, avs, avr, aps, apr, ps, pr, rs, rr, yys, yyr, vs, vr,
):
    p = lax.axis_index("pipe")
    v = lax.axis_index("vocab")
    zz = lax.rem(p, 8)
    yh = p // 8
    core = lax.rem(v, 2)
    mate = v + 1 - 2 * core
    other_y = lax.rem(p + 8, 16)
    zup = yh * 8 + lax.rem(zz + 1, 8)
    zdn = yh * 8 + lax.rem(zz + 7, 8)
    wcopy = pltpu.make_async_copy(w_hbm, w, w_sem)
    wcopy.start()

    bar = pltpu.get_barrier_semaphore()

    @pl.loop(1, 16)
    def _(i):
        pl.semaphore_signal(bar, inc=1, device_id=(p, lax.rem(v + i, 16)), device_id_type=MESH)
        pl.semaphore_signal(bar, inc=1, device_id=(lax.rem(p + i, 16), v), device_id_type=MESH)

    pl.semaphore_wait(bar, 30)

    bufs = (h_buf, c_buf)
    ins = (h_in, c_in)

    def s1copy(a, i):
        return rcopy(ins[a], s1.at[a, v], s1s.at[a, i], s1r.at[a, i], p, lax.rem(v + i, 16))

    for a in range(2):
        @pl.loop(1, 16)
        def _(i):
            s1copy(a, i).start()
    cols = pl.ds(pl.multiple_of(core * HALF, 128), HALF)
    mate_cols = pl.ds(pl.multiple_of((1 - core) * HALF, 128), HALF)
    s1[0, pl.ds(v, 1)] = h_in[...][None]
    s1[1, pl.ds(v, 1)] = c_in[...][None]

    def s1_finish(a):
        @pl.loop(1, 16)
        def _(i):
            s1copy(a, i).wait_recv()
        bufs[a][yh, zz] = jnp.concatenate([s1[a, k] for k in range(16)], axis=-1)

    def blk(a, y, z):
        return bufs[a].at[y, z, :, cols]

    def ycopy(a):
        return rcopy(blk(a, yh, zz), blk(a, yh, zz), ys.at[a], yr.at[a], other_y, v)

    def zcopy(a, d, s, k):
        y = yh if k == 0 else 1 - yh
        z = lax.rem(zz - s + 8, 8) if d == 0 else lax.rem(zz + s, 8)
        return rcopy(blk(a, y, z), blk(a, y, z), zs.at[a, d, s, k], zr.at[a, d, s, k], zup if d == 0 else zdn, v)

    def mcopy(a, y, z):
        return rcopy(blk(a, y, z), blk(a, y, z), cs.at[a, y, z], cr.at[a, y, z], p, mate)

    def has(d, s, k):
        return s < 3 or k == d

    def arrived(d, s, k):
        y = yh if k == 0 else 1 - yh
        z = lax.rem(zz - s - 1 + 8, 8) if d == 0 else lax.rem(zz + s + 1, 8)
        return y, z

    def ring_begin(a):
        ycopy(a).start()
        for d in range(2):
            zcopy(a, d, 0, 0).start()

    def ring_second(a):
        ycopy(a).wait_recv()
        for d in range(2):
            zcopy(a, d, 0, 1).start()
        mcopy(a, 1 - yh, zz).start()

    def ring_step(a, s):
        for k in range(2):
            for d in range(2):
                if has(d, s, k):
                    zcopy(a, d, s, k).wait_recv()
                    if s < 3 and has(d, s + 1, k):
                        zcopy(a, d, s + 1, k).start()
                    mcopy(a, *arrived(d, s, k)).start()

    def ring_finish(a):
        mcopy(a, 1 - yh, zz).wait_recv()
        for s in range(4):
            for k in range(2):
                for d in range(2):
                    if has(d, s, k):
                        mcopy(a, *arrived(d, s, k)).wait_recv()

    def ring_drain(a):
        ycopy(a).wait_send()
        mcopy(a, 1 - yh, zz).wait_send()
        for s in range(4):
            for k in range(2):
                for d in range(2):
                    if has(d, s, k):
                        mcopy(a, *arrived(d, s, k)).wait_send()
                        zcopy(a, d, s, k).wait_send()

        @pl.loop(1, 16)
        def _(i):
            s1copy(a, i).wait_send()

    s1_finish(0)
    ring_begin(0)
    ring_second(0)
    s1_finish(1)
    for s in range(4):
        ring_step(0, s)
    ring_begin(1)
    ring_finish(0)
    ring_second(1)
    wcopy.wait()

    base = (p * 16 + v) * ROWS
    tgt = tgt_ref[...]

    def row_ids(i, rows):
        return base + i * rows + lax.broadcasted_iota(jnp.int32, (rows, TOKENS), 0)

    ar_src[...] = jnp.zeros_like(ar_src)

    @pl.loop(0, 5)
    def _(i):
        r = pl.ds(pl.multiple_of(i * 128, 128), 128)
        logits = lax.dot_general(w[r, :], h_buf[...].reshape(TOKENS, D), NT, preferred_element_type=F32)
        t = jnp.tanh(logits / 30.0)
        tanh_buf[r, :] = t
        capped = 30.0 * t
        ar_src[0:1, :] += jnp.sum(jnp.exp(capped), axis=0, keepdims=True)
        ar_src[1:2, :] += jnp.sum(jnp.where(row_ids(i, 128) == tgt, capped, 0.0), axis=0, keepdims=True)

    def avcopy(i):
        return rcopy(ar_src, ar_v.at[v], avs.at[i], avr.at[i], p, lax.rem(v + i, 16))

    def apcopy(i):
        return rcopy(ar_src, ar_p.at[p], aps.at[i], apr.at[i], lax.rem(p + i, 16), v)

    @pl.loop(1, 16)
    def _(i):
        avcopy(i).start()
    ar_v[pl.ds(v, 1)] = ar_src[...][None]

    @pl.loop(1, 16)
    def _(i):
        avcopy(i).wait()
    ar_src[...] = jnp.sum(ar_v[...], axis=0)

    @pl.loop(1, 16)
    def _(i):
        apcopy(i).start()
    ar_p[pl.ds(p, 1)] = ar_src[...][None]

    @pl.loop(1, 16)
    def _(i):
        apcopy(i).wait()
    sums = jnp.sum(ar_p[...], axis=0)
    sum_exp = sums[0:1, :]
    loss_out[...] = jnp.log(sum_exp) - sums[1:2, :]

    @pl.loop(0, 5)
    def _(i):
        r = pl.ds(pl.multiple_of(i * 128, 128), 128)
        t = tanh_buf[r, :]
        hit = (row_ids(i, 128) == tgt).astype(F32)
        d = (jnp.exp(30.0 * t) / sum_exp - hit) * (1.0 - t * t)
        dlt[r, :] = d.astype(BF)
        dl[:, r] = d.T.astype(BF)

    ring_step(1, 0)

    @pl.loop(0, 9)
    def _(i):
        n = pl.ds(pl.multiple_of(i * 512, 512), 512)
        g = jnp.dot(dl[...], w[:, n], preferred_element_type=F32)
        g_buf[:, :, :, n] = g.astype(BF).reshape(2, 8, 32, 512)

    ring_step(1, 1)
    ring_step(1, 2)
    ring_step(1, 3)

    def pcopy(j):
        z = lax.rem(zz + j, 8)
        return rcopy(g_buf.at[:, z, :, mate_cols], pair.at[:, z], ps.at[j], pr.at[j], p, mate)

    order = (4, 3, 5, 2, 6, 1, 7, 0)
    for j in order:
        pcopy(j).start()

    def rdest(d, s):
        return lax.rem(zz + 4 - s, 8) if d == 0 else lax.rem(zz + 4 + s, 8)

    def rsend(d, s, y):
        z = rdest(d, s)
        return rcopy(pair.at[y, z], rbuf.at[d, s, y], rs.at[d, s, y], rr.at[d, s, y], zup if d == 0 else zdn, v)

    def rhas(d, s, y):
        return s > 0 or y == d

    def own(y, z):
        return g_buf[y, z, :, cols].astype(F32) + pair[y, z].astype(F32)

    for s in range(4):
        for d in range(2):
            if s == 0:
                if d == 0:
                    pcopy(4).wait_recv()
            else:
                pcopy(4 - s if d == 0 else 4 + s).wait_recv()
            for y in range(2):
                if rhas(d, s, y):
                    total = own(y, rdest(d, s))
                    if s > 0 and rhas(d, s - 1, y):
                        rsend(d, s - 1, y).wait_recv()
                        total += rbuf[d, s - 1, y].astype(F32)
                    pair[y, rdest(d, s)] = total.astype(BF)
                    rsend(d, s, y).start()

    ring_finish(1)

    @pl.loop(0, 9)
    def _(i):
        n = pl.ds(pl.multiple_of(i * 512, 512), 512)
        sel = (
            base + lax.broadcasted_iota(jnp.int32, (ROWS, TOKENS), 0) == ids_ref[...]
        ).astype(F32).astype(BF)
        acc = jnp.dot(sel, c_buf[:, :, :, n].reshape(TOKENS, 512), preferred_element_type=F32) * (float(D) ** 0.5)
        acc += jnp.dot(dlt[...], h_buf[:, :, :, n].reshape(TOKENS, 512), preferred_element_type=F32)
        grad_out[:, n] = acc.astype(BF)

    pcopy(0).wait_recv()

    def final(y):
        total = own(y, zz)
        for d in range(2):
            total += rbuf[d, 3, y].astype(F32)
        return total

    for d in range(2):
        for y in range(2):
            rsend(d, 3, y).wait_recv()
    ycp = rcopy(y_buf.at[0], y_buf.at[1], yys, yyr, other_y, v)
    y_buf[0] = final(1 - yh).astype(BF)
    ycp.start()
    mine = final(yh)
    ycp.wait()
    mine += y_buf[1].astype(F32)

    def vcopy(k):
        return rcopy(v_src.at[k], v_buf.at[v // 2], vs.at[k], vr.at[v // 2], p, core * 8 + k)

    for k in range(8):
        v_src[k] = mine[:, k * PIECE : (k + 1) * PIECE]
    for k in range(8):
        @pl.when(core * 8 + k != v)
        def _():
            vcopy(k).start()

        @pl.when(core * 8 + k == v)
        def _():
            v_buf[pl.ds(v // 2, 1)] = v_src[k][None]
    for j in range(8):
        @pl.when(2 * j + v // 8 != v)
        def _():
            rcopy(v_src.at[0], v_buf.at[j], vs.at[0], vr.at[j], p, mate).wait_recv()
    hid_out[...] = jnp.sum(v_buf[...], axis=0)

    for k in range(8):
        @pl.when(core * 8 + k != v)
        def _():
            vcopy(k).wait_send()
    for a in range(2):
        ring_drain(a)
    for j in order:
        pcopy(j).wait_send()
    for s in range(4):
        for d in range(2):
            for y in range(2):
                if rhas(d, s, y):
                    rsend(d, s, y).wait_send()


def local(final_hidden, tied_table, target_ids, input_ids, embed_cot):
    vm = pl.BlockSpec(memory_space=pltpu.VMEM)
    sem = pltpu.SemaphoreType.DMA
    grad, hid, loss = pl.pallas_call(
        kernel,
        out_shape=[
            jax.ShapeDtypeStruct((ROWS, D), BF),
            jax.ShapeDtypeStruct((32, PIECE), F32),
            jax.ShapeDtypeStruct((1, TOKENS), F32),
        ],
        in_specs=[vm, pl.BlockSpec(memory_space=pl.ANY), vm, vm, vm],
        out_specs=[vm, vm, vm],
        scratch_shapes=[
            pltpu.VMEM((ROWS, D), BF),
            pltpu.VMEM((2, 8, 32, D), BF),
            pltpu.VMEM((2, 8, 32, D), BF),
            pltpu.VMEM((ROWS, TOKENS), F32),
            pltpu.VMEM((TOKENS, ROWS), BF),
            pltpu.VMEM((ROWS, TOKENS), BF),
            pltpu.VMEM((2, 8, 32, HALF), BF),
            pltpu.VMEM((2, 4, 2, 32, HALF), BF),
            pltpu.VMEM((2, 8, 32, D), BF),
            pltpu.VMEM((2, 16, 32, PIECE), BF),
            pltpu.VMEM((8, TOKENS), F32),
            pltpu.VMEM((16, 8, TOKENS), F32),
            pltpu.VMEM((16, 8, TOKENS), F32),
            pltpu.VMEM((2, 32, HALF), BF),
            pltpu.VMEM((8, 32, PIECE), F32),
            pltpu.VMEM((8, 32, PIECE), F32),
            sem, sem((2, 16)), sem((2, 16)), sem((2,)), sem((2,)),
            sem((2, 2, 4, 2)), sem((2, 2, 4, 2)), sem((2, 2, 8)), sem((2, 2, 8)),
            sem((16,)), sem((16,)), sem((16,)), sem((16,)),
            sem((8,)), sem((8,)), sem((2, 4, 2)), sem((2, 4, 2)), sem, sem, sem((8,)), sem((8,)),
        ],
        compiler_params=pltpu.CompilerParams(
            collective_id=0, has_side_effects=True, vmem_limit_bytes=63 << 20
        ),
        name="head_backward",
    )(
        final_hidden,
        tied_table,
        target_ids.reshape(1, TOKENS),
        input_ids.reshape(1, TOKENS),
        embed_cot,
    )
    held = final_hidden.shape[0]
    loss_shard = lax.dynamic_slice_in_dim(loss[0], lax.axis_index("pipe") * held, held)
    return (grad, hid, loss_shard)


def solution(mesh):
    placed = (P("pipe", "vocab"), P(("pipe", "vocab"), None), P(), P(), P("pipe", "vocab"))
    return jax.shard_map(
        local,
        mesh=mesh,
        in_specs=placed,
        out_specs=(P(("pipe", "vocab"), None), P("pipe", "vocab"), P("pipe")),
        check_vma=False,
    )
```

```python
import jax
import jax.numpy as jnp
from jax import lax
from jax.experimental import pallas as pl
from jax.experimental.pallas import tpu as pltpu
from jax.sharding import PartitionSpec as P

D = 4608
HALF = D // 2
QUART = D // 4
LAG = 5
RLAG = 3
SLOTS = 15 + 2 * LAG
ROWS = 640
TOKENS = 512
PIECE = 288
BF = jnp.bfloat16
F32 = jnp.float32
MESH = pl.DeviceIdType.MESH
NT = (((1,), (1,)), ((), ()))


def rcopy(src, dst, send, recv, p, v):
    return pltpu.make_async_remote_copy(
        src_ref=src, dst_ref=dst, send_sem=send, recv_sem=recv, device_id=(p, v), device_id_type=MESH
    )


def kernel(
    h_in, w_hbm, tgt_ref, ids_ref, c_in,
    grad_out, hid_out, loss_out,
    w, h_buf, c_buf, tanh_buf, dl, dlt, pair, rbuf, g_buf,
    s1, ar_src, ar_v, ar_p, y_buf, v_src, v_buf,
    xr1, xr2,
    w_sem, s1s, s1r, ys, yr, zs, zr, cs, cr, avs, avr, aps, apr, ps, pr, rs, rr, yys, yyr, vs, vr,
    xs, xr, x1s, x1r, x2s, x2r, gs, g_stage,
):
    p = lax.axis_index("pipe")
    v = lax.axis_index("vocab")
    zz = lax.rem(p, 8)
    yh = p // 8
    core = lax.rem(v, 2)
    mate = v + 1 - 2 * core
    xx = lax.rem(v // 2, 4)
    ylo = v // 8
    x_at = lambda i: lax.rem(xx + i, 4)
    x_dev = lambda i: ylo * 8 + x_at(i) * 2 + core
    other_y = lax.rem(p + 8, 16)
    zup = yh * 8 + lax.rem(zz + 1, 8)
    zdn = yh * 8 + lax.rem(zz + 7, 8)
    wcopy = pltpu.make_async_copy(w_hbm, w, w_sem)
    wcopy.start()

    bar = pltpu.get_barrier_semaphore()

    @pl.loop(1, 16)
    def _(i):
        pl.semaphore_signal(bar, inc=1, device_id=(p, lax.rem(v + i, 16)), device_id_type=MESH)
        pl.semaphore_signal(bar, inc=1, device_id=(lax.rem(p + i, 16), v), device_id_type=MESH)

    pl.semaphore_wait(bar, 30)

    bufs = (h_buf, c_buf)
    ins = (h_in, c_in)

    def s1dev(i):
        return lax.rem(v // 2 + i, 8) * 2 + ylo

    def s1copy(a, i):
        return rcopy(ins[a], s1.at[a, lax.rem(v, 8)], s1s.at[a, i], s1r.at[a, lax.rem(v, 8)], p, s1dev(i))

    def s1_begin(a):
        @pl.loop(1, 8)
        def _(i):
            s1copy(a, i).start()

        @pl.when(core != ylo)
        def _():
            s1copy(a, 0).start()

        @pl.when(core == ylo)
        def _():
            s1[a, pl.ds(lax.rem(v, 8), 1)] = ins[a][...][None]

    mate_cols = pl.ds(pl.multiple_of((1 - core) * HALF, 128), HALF)

    def s1_finish(a):
        @pl.loop(0, 8)
        def _(j):
            @pl.when(core * 8 + j != v)
            def _():
                rcopy(ins[a], s1.at[a, j], s1s.at[a, 0], s1r.at[a, j], p, mate).wait_recv()

        block = jnp.concatenate([s1[a, k] for k in range(8)], axis=-1)
        for c in range(2):
            @pl.when(core == c)
            def _():
                bufs[a][yh, zz, :, c * HALF : (c + 1) * HALF] = block

    def s1_drain(a):
        @pl.loop(1, 8)
        def _(i):
            s1copy(a, i).wait_send()

        @pl.when(core != ylo)
        def _():
            s1copy(a, 0).wait_send()

    s1_begin(0)

    def piece(ref, y, z, x):
        return ref.at[
            y, z, pl.ds(pl.multiple_of(lax.rem(x, 2) * 16, 16), 16), pl.ds(pl.multiple_of(x // 2 * QUART, 128), QUART)
        ]

    def part(ref, c, y, z):
        return piece(ref, y, z, xx) if c == 0 else ref.at[y, z, :, pl.ds(HALF, HALF)]

    def ycopy(c, a):
        b = part(bufs[a], c, yh, zz)
        return rcopy(b, b, ys.at[a], yr.at[a], other_y, v)

    def zcopy(c, a, d, s, k):
        y = yh if k == 0 else 1 - yh
        z = lax.rem(zz - s + 8, 8) if d == 0 else lax.rem(zz + s, 8)
        b = part(bufs[a], c, y, z)
        return rcopy(b, b, zs.at[a, d, s, k], zr.at[a, d, s, k], zup if d == 0 else zdn, v)

    def mcopy(c, a, y, z):
        b = bufs[a].at[y, z, :, pl.ds(c * HALF, HALF)]
        return rcopy(b, b, cs.at[a, y, z], cr.at[a, y, z], p, mate)

    def xcopy(a, d, hop, y, z):
        b = piece(bufs[a], y, z, xx if hop == 0 else x_at(3 if d == 0 else 1))
        return rcopy(b, b, xs.at[a, d, hop, y, z], xr.at[a, d, hop, y, z], p, x_dev(1 if d == 0 else 3))

    def has(d, s, k):
        return s < 3 or k == d

    events = [None] + [(s, k, d) for s in range(4) for k in range(2) for d in range(2) if has(d, s, k)]

    def where(e):
        if e is None:
            return 1, 1 - yh, zz
        s, k, d = e
        z = lax.rem(zz - s - 1 + 8, 8) if d == 0 else lax.rem(zz + s + 1, 8)
        return k, (yh if k == 0 else 1 - yh), z

    def on_core(c):
        return pl.when(core == c)

    def ring_begin(a):
        for c in range(2):
            @on_core(c)
            def _():
                ycopy(c, a).start()
                for d in range(2):
                    zcopy(c, a, d, 0, 0).start()
                mcopy(c, a, yh, zz).start()

    def take(c, a, e):
        k, y, z = where(e)
        if e is None:
            ycopy(c, a).wait_recv()
            for d in range(2):
                zcopy(c, a, d, 0, 1).start()
        else:
            s, k, d = e
            zcopy(c, a, d, s, k).wait_recv()
            if s < 3 and has(d, s + 1, k):
                zcopy(c, a, d, s + 1, k).start()
        if c == 1:
            mcopy(c, a, y, z).start()
        else:
            for d in range(2):
                xcopy(a, d, 0, y, z).start()

    def ring_slots(a, lo, hi):
        @on_core(0)
        def _():
            for i in range(lo, hi):
                if i < 15:
                    take(0, a, events[i])
                if LAG <= i < 15 + LAG:
                    k, y, z = where(events[i - LAG])
                    for d in range(2):
                        xcopy(a, d, 0, y, z).wait_recv()
                    xcopy(a, k, 1, y, z).start()
                if i >= 2 * LAG:
                    k, y, z = where(events[i - 2 * LAG])
                    xcopy(a, k, 1, y, z).wait_recv()
                    mcopy(0, a, y, z).start()

        @on_core(1)
        def _():
            for i in range(min(lo, 15), min(hi, 15)):
                take(1, a, events[i])

    def ring_finish(a):
        for c in range(2):
            @on_core(c)
            def _():
                mcopy(1 - c, a, yh, zz).wait_recv()
                for e in events:
                    _, y, z = where(e)
                    mcopy(1 - c, a, y, z).wait_recv()

    def ring_drain(a):
        for c in range(2):
            @on_core(c)
            def _():
                ycopy(c, a).wait_send()
                mcopy(c, a, yh, zz).wait_send()
                for e in events:
                    k, y, z = where(e)
                    mcopy(c, a, y, z).wait_send()
                    if c == 0:
                        for d in range(2):
                            xcopy(a, d, 0, y, z).wait_send()
                        xcopy(a, k, 1, y, z).wait_send()
                    if e is not None:
                        s, k, d = e
                        zcopy(c, a, d, s, k).wait_send()

        s1_drain(a)

    s1_finish(0)
    ring_begin(0)
    s1_begin(1)
    ring_slots(0, 0, 9)
    s1_finish(1)
    ring_slots(0, 9, SLOTS)
    ring_begin(1)
    ring_finish(0)
    wcopy.wait()

    base = (p * 16 + v) * ROWS
    tgt = tgt_ref[...]

    def row_ids(i, rows):
        return base + i * rows + lax.broadcasted_iota(jnp.int32, (rows, TOKENS), 0)

    ar_src[...] = jnp.zeros_like(ar_src)

    for i in range(5):
        r = slice(i * 128, (i + 1) * 128)
        logits = lax.dot_general(w[r, :], h_buf[...].reshape(TOKENS, D), NT, preferred_element_type=F32)
        t = jnp.tanh(logits / 30.0)
        tanh_buf[r, :] = t
        capped = 30.0 * t
        ar_src[0:1, :] += jnp.sum(jnp.exp(capped), axis=0, keepdims=True)
        ar_src[1:2, :] += jnp.sum(jnp.where(row_ids(i, 128) == tgt, capped, 0.0), axis=0, keepdims=True)
        ring_slots(1, 2 * i, 2 * i + 2)

    def avcopy(i):
        return rcopy(ar_src, ar_v.at[v], avs.at[i], avr.at[i], p, lax.rem(v + i, 16))

    def apcopy(i):
        return rcopy(ar_src, ar_p.at[p], aps.at[i], apr.at[i], lax.rem(p + i, 16), v)

    @pl.loop(1, 16)
    def _(i):
        avcopy(i).start()
    ar_v[pl.ds(v, 1)] = ar_src[...][None]
    ring_slots(1, 10, 14)

    @pl.loop(1, 16)
    def _(i):
        avcopy(i).wait()
    ar_src[...] = jnp.sum(ar_v[...], axis=0)

    @pl.loop(1, 16)
    def _(i):
        apcopy(i).start()
    ar_p[pl.ds(p, 1)] = ar_src[...][None]
    ring_slots(1, 14, 20)

    @pl.loop(1, 16)
    def _(i):
        apcopy(i).wait()
    sums = jnp.sum(ar_p[...], axis=0)
    sum_exp = sums[0:1, :]
    loss_out[...] = jnp.log(sum_exp) - sums[1:2, :]

    @pl.loop(0, 5)
    def _(i):
        r = pl.ds(pl.multiple_of(i * 128, 128), 128)
        t = tanh_buf[r, :]
        hit = (row_ids(i, 128) == tgt).astype(F32)
        d = (jnp.exp(30.0 * t) / sum_exp - hit) * (1.0 - t * t)
        dlt[r, :] = d.astype(BF)
        dl[:, r] = d.T.astype(BF)

    ring_slots(1, 20, SLOTS)

    def products(half):
        @pl.loop(0, 3)
        def _(i):
            n = pl.ds(pl.multiple_of(half * HALF + i * 768, 128), 768)
            g = jnp.dot(dl[...], w[:, n], preferred_element_type=F32)
            g_buf[:, :, :, n] = g.astype(BF).reshape(2, 8, 32, 768)

    def pcopy(j):
        z = lax.rem(zz + j, 8)
        return rcopy(g_buf.at[:, z, :, mate_cols], pair.at[:, z], ps.at[j], pr.at[j], p, mate)

    order = (4, 3, 5, 2, 6, 1, 7, 0)
    products(1 - core)
    for j in order:
        pcopy(j).start()
    products(core)

    def paired(y, z, c):
        return g_buf[y, z, :, pl.ds(c * HALF, HALF)].astype(F32) + pair[y, z].astype(F32)

    def rdest(d, s):
        return lax.rem(zz + 4 - s, 8) if d == 0 else lax.rem(zz + 4 + s, 8)

    def jdest(d, s):
        return 4 - s if d == 0 else lax.rem(4 + s, 8)

    def rpart(ref, c, *at):
        return ref.at[(*at, pl.ds(0, 16), pl.ds(0, QUART))] if c == 0 else ref.at[at]

    def rsend(c, d, s, y):
        z = rdest(d, s)
        src = piece(pair, y, z, xx) if c == 0 else pair.at[y, z]
        return rcopy(src, rpart(rbuf, c, d, s, y), rs.at[d, s, y], rr.at[d, s, y], zup if d == 0 else zdn, v)

    def rhas(d, s, y):
        return s > 0 or y == d

    def rstep(c, d, s, total_of):
        for y in range(2):
            if rhas(d, s, y):
                z = rdest(d, s)
                total = total_of(y, jdest(d, s))
                if s > 0 and rhas(d, s - 1, y):
                    rsend(c, d, s - 1, y).wait_recv()
                    total += rpart(rbuf, c, d, s - 1, y)[...].astype(F32)
                (piece(pair, y, z, xx) if c == 0 else pair.at[y, z])[...] = total.astype(BF)
                rsend(c, d, s, y).start()

    def zof(j):
        return lax.rem(zz + j, 8)

    def x1copy(y, j):
        z = zof(j)
        return rcopy(piece(pair, y, z, x_at(2)), xr1.at[y, z], x1s.at[y, z], x1r.at[y, z], p, x_dev(1 if y == 0 else 3))

    def x2copy(d, y, j):
        z = zof(j)
        to = 1 if d == 0 else 3
        return rcopy(piece(pair, y, z, x_at(to)), xr2.at[d, y, z], x2s.at[d, y, z], x2r.at[d, y, z], p, x_dev(to))

    def xtotal(y, j):
        z = zof(j)
        return piece(pair, y, z, xx)[...].astype(F32) + xr2[0, y, z].astype(F32) + xr2[1, y, z].astype(F32)

    blocks = [(y, j) for j in order for y in range(2)]
    zsteps = {4: [(0, 0), (1, 0)], 3: [(0, 1)], 5: [(1, 1)], 2: [(0, 2)], 6: [(1, 2)], 1: [(0, 3)], 7: [(1, 3)], 0: []}

    def reduce0(i):
        if i < 16:
            y, j = blocks[i]
            if y == 0:
                pcopy(j).wait_recv()
            pair[y, zof(j)] = paired(y, zof(j), 0).astype(BF)
            x1copy(y, j).start()
        if RLAG <= i < 16 + RLAG:
            y, j = blocks[i - RLAG]
            x1copy(y, j).wait_recv()
            b = piece(pair, y, zof(j), x_at(1 if y == 0 else 3))
            b[...] = (b[...].astype(F32) + xr1[y, zof(j)].astype(F32)).astype(BF)
            for d in range(2):
                x2copy(d, y, j).start()
        if i >= 2 * RLAG:
            y, j = blocks[i - 2 * RLAG]
            for d in range(2):
                x2copy(d, y, j).wait_recv()
            if y == 1:
                for d, s in zsteps[j]:
                    rstep(0, d, s, xtotal)

    def reduce1(i):
        j = order[i]
        pcopy(j).wait_recv()
        for d, s in zsteps[j]:
            rstep(1, d, s, lambda y, j: paired(y, zof(j), 1))

    def gcopy(i):
        return pltpu.make_async_copy(g_stage.at[i % 2], grad_out.at[:, i * 512 : (i + 1) * 512], gs.at[i % 2])

    def table(i):
        n = slice(i * 512, (i + 1) * 512)
        sel = (
            base + lax.broadcasted_iota(jnp.int32, (ROWS, TOKENS), 0) == ids_ref[...]
        ).astype(F32).astype(BF)
        acc = jnp.dot(sel, c_buf[:, :, :, n].reshape(TOKENS, 512), preferred_element_type=F32) * (float(D) ** 0.5)
        acc += jnp.dot(dlt[...], h_buf[:, :, :, n].reshape(TOKENS, 512), preferred_element_type=F32)
        if i >= 2:
            gcopy(i - 2).wait()
        g_stage[i % 2] = acc.astype(BF)
        gcopy(i).start()

    ring_finish(1)
    for i in range(16 + 2 * RLAG):
        @on_core(0)
        def _():
            reduce0(i)

        if i % 2 == 0 and i < 16:
            @on_core(1)
            def _():
                reduce1(i // 2)

        if i % 2 == 0 and i < 18:
            table(i // 2)

    def last(c, y):
        total = xtotal(y, 0) if c == 0 else paired(y, zz, 1)
        for d in range(2):
            total += rpart(rbuf, c, d, 3, y)[...].astype(F32)
        return total

    def yback(c):
        return rcopy(rpart(y_buf, c, 0), rpart(y_buf, c, 1), yys, yyr, other_y, v)

    def owner(c, k):
        return xx // 2 * 4 + k if c == 0 else 8 + k

    def vcopy(c, k):
        slot = ylo * 2 + lax.rem(xx, 2) if c == 0 else v // 2
        if c == 0:
            return rcopy(v_src.at[k, pl.ds(0, 16)], v_buf.at[slot, pl.ds(0, 16)], vs.at[k], vr.at[slot], p, owner(c, k))
        return rcopy(v_src.at[k], v_buf.at[slot], vs.at[k], vr.at[slot], p, owner(c, k))

    for c in range(2):
        @on_core(c)
        def _():
            for d in range(2):
                for y in range(2):
                    rsend(c, d, 3, y).wait_recv()
            rpart(y_buf, c, 0)[...] = last(c, 1 - yh).astype(BF)
            yback(c).start()
            mine = last(c, yh)
            yback(c).wait()
            mine += rpart(y_buf, c, 1)[...].astype(F32)
            rows = 16 if c == 0 else 32
            count = 4 if c == 0 else 8
            for k in range(count):
                v_src[k, 0:rows] = mine[:, k * PIECE : (k + 1) * PIECE]
            for k in range(count):
                @pl.when(owner(c, k) != v)
                def _():
                    vcopy(c, k).start()

                @pl.when(owner(c, k) == v)
                def _():
                    slot = ylo * 2 + lax.rem(xx, 2) if c == 0 else v // 2
                    v_buf[pl.ds(slot, 1), 0:rows] = v_src[k, 0:rows][None]

    @pl.when(v < 8)
    def _():
        for j in range(4):
            @pl.when((j // 2) * 8 + (v // 4 * 2 + j % 2) * 2 != v)
            def _():
                b = v_buf.at[j, pl.ds(0, 16)]
                rcopy(v_src.at[0, pl.ds(0, 16)], b, vs.at[0], vr.at[j], p, mate).wait_recv()
        for r in range(2):
            hid_out[16 * r : 16 * r + 16, :] = v_buf[r, 0:16] + v_buf[2 + r, 0:16]

    @pl.when(v >= 8)
    def _():
        for j in range(8):
            @pl.when(2 * j + 1 != v)
            def _():
                rcopy(v_src.at[0], v_buf.at[j], vs.at[0], vr.at[j], p, mate).wait_recv()
        hid_out[...] = jnp.sum(v_buf[...], axis=0)

    gcopy(7).wait()
    gcopy(8).wait()
    for a in range(2):
        ring_drain(a)
    for j in order:
        pcopy(j).wait_send()
    for c in range(2):
        @on_core(c)
        def _():
            for k in range(4 if c == 0 else 8):
                @pl.when(owner(c, k) != v)
                def _():
                    vcopy(c, k).wait_send()
            for s in range(4):
                for d in range(2):
                    for y in range(2):
                        if rhas(d, s, y):
                            rsend(c, d, s, y).wait_send()
            if c == 0:
                for y, j in blocks:
                    x1copy(y, j).wait_send()
                    for d in range(2):
                        x2copy(d, y, j).wait_send()


def local(final_hidden, tied_table, target_ids, input_ids, embed_cot):
    vm = pl.BlockSpec(memory_space=pltpu.VMEM)
    sem = pltpu.SemaphoreType.DMA
    grad, hid, loss = pl.pallas_call(
        kernel,
        out_shape=[
            jax.ShapeDtypeStruct((ROWS, D), BF),
            jax.ShapeDtypeStruct((32, PIECE), F32),
            jax.ShapeDtypeStruct((1, TOKENS), F32),
        ],
        in_specs=[vm, pl.BlockSpec(memory_space=pl.ANY), vm, vm, vm],
        out_specs=[pl.BlockSpec(memory_space=pl.ANY), vm, vm],
        scratch_shapes=[
            pltpu.VMEM((ROWS, D), BF),
            pltpu.VMEM((2, 8, 32, D), BF),
            pltpu.VMEM((2, 8, 32, D), BF),
            pltpu.VMEM((ROWS, TOKENS), F32),
            pltpu.VMEM((TOKENS, ROWS), BF),
            pltpu.VMEM((ROWS, TOKENS), BF),
            pltpu.VMEM((2, 8, 32, HALF), BF),
            pltpu.VMEM((2, 4, 2, 32, HALF), BF),
            pltpu.VMEM((2, 8, 32, D), BF),
            pltpu.VMEM((2, 8, 32, PIECE), BF),
            pltpu.VMEM((8, TOKENS), F32),
            pltpu.VMEM((16, 8, TOKENS), F32),
            pltpu.VMEM((16, 8, TOKENS), F32),
            pltpu.VMEM((2, 32, HALF), BF),
            pltpu.VMEM((8, 32, PIECE), F32),
            pltpu.VMEM((8, 32, PIECE), F32),
            pltpu.VMEM((2, 8, 16, QUART), BF),
            pltpu.VMEM((2, 2, 8, 16, QUART), BF),
            sem, sem((2, 8)), sem((2, 8)), sem((2,)), sem((2,)),
            sem((2, 2, 4, 2)), sem((2, 2, 4, 2)), sem((2, 2, 8)), sem((2, 2, 8)),
            sem((16,)), sem((16,)), sem((16,)), sem((16,)),
            sem((8,)), sem((8,)), sem((2, 4, 2)), sem((2, 4, 2)), sem, sem, sem((8,)), sem((8,)),
            sem((2, 2, 2, 2, 8)), sem((2, 2, 2, 2, 8)), sem((2, 8)), sem((2, 8)), sem((2, 2, 8)), sem((2, 2, 8)), sem((2,)), pltpu.VMEM((2, ROWS, 512), BF),
        ],
        compiler_params=pltpu.CompilerParams(
            collective_id=0, has_side_effects=True, vmem_limit_bytes=63 << 20
        ),
        name="head_backward",
    )(
        final_hidden,
        tied_table,
        target_ids.reshape(1, TOKENS),
        input_ids.reshape(1, TOKENS),
        embed_cot,
    )
    held = final_hidden.shape[0]
    loss_shard = lax.dynamic_slice_in_dim(loss[0], lax.axis_index("pipe") * held, held)
    return (grad, hid, loss_shard)


def solution(mesh):
    placed = (P("pipe", "vocab"), P(("pipe", "vocab"), None), P(), P(), P("pipe", "vocab"))
    return jax.shard_map(
        local,
        mesh=mesh,
        in_specs=placed,
        out_specs=(P(("pipe", "vocab"), None), P("pipe", "vocab"), P("pipe")),
        check_vma=False,
    )
```

```python
import jax
import jax.numpy as jnp
from jax import lax
from jax.experimental import pallas as pl
from jax.experimental.pallas import tpu as pltpu
from jax.sharding import PartitionSpec as P

D = 4608
HALF = D // 2
QUART = D // 4
LAG = 5
RLAG = 3
SLOTS = 15 + 2 * LAG
ROWS = 640
TOKENS = 512
PIECE = 288
BF = jnp.bfloat16
F32 = jnp.float32
MESH = pl.DeviceIdType.MESH
NT = (((1,), (1,)), ((), ()))


def rcopy(src, dst, send, recv, p, v):
    return pltpu.make_async_remote_copy(
        src_ref=src, dst_ref=dst, send_sem=send, recv_sem=recv, device_id=(p, v), device_id_type=MESH
    )


def kernel(
    h_in, w_hbm, tgt_ref, ids_ref, c_in,
    grad_out, hid_out, loss_out,
    w, h_buf, c_buf, tanh_buf, dl, dlt, pair, rbuf, g_buf,
    s1, sums, ar_src, ar_v, ar_p, y_buf, v_src, v_buf,
    xr1, xr2,
    w_sem, s1s, s1r, ys, yr, zs, zr, cs, cr, avs, avr, aps, apr, ps, pr, rs, rr, yys, yyr, vs, vr,
    xs, xr, x1s, x1r, x2s, x2r, gs, g_stage,
):
    p = lax.axis_index("pipe")
    v = lax.axis_index("vocab")
    zz = lax.rem(p, 8)
    yh = p // 8
    core = lax.rem(v, 2)
    mate = v + 1 - 2 * core
    xx = lax.rem(v // 2, 4)
    ylo = v // 8
    x_at = lambda i: lax.rem(xx + i, 4)
    x_dev = lambda i: ylo * 8 + x_at(i) * 2 + core
    other_y = lax.rem(p + 8, 16)
    zup = yh * 8 + lax.rem(zz + 1, 8)
    zdn = yh * 8 + lax.rem(zz + 7, 8)
    wcopy = pltpu.make_async_copy(w_hbm, w, w_sem)
    wcopy.start()

    bar = pltpu.get_barrier_semaphore()

    @pl.loop(1, 16)
    def _(i):
        pl.semaphore_signal(bar, inc=1, device_id=(p, lax.rem(v + i, 16)), device_id_type=MESH)

    for q in (other_y, zup, zdn):
        pl.semaphore_signal(bar, inc=1, device_id=(q, v), device_id_type=MESH)
    pl.semaphore_wait(bar, 18)

    bufs = (h_buf, c_buf)
    ins = (h_in, c_in)

    def s1dev(i):
        return lax.rem(v // 2 + i, 8) * 2 + ylo

    def s1copy(a, i):
        return rcopy(ins[a], s1.at[a, lax.rem(v, 8)], s1s.at[a, i], s1r.at[a, lax.rem(v, 8)], p, s1dev(i))

    def s1_begin(a):
        @pl.loop(1, 8)
        def _(i):
            s1copy(a, i).start()

        @pl.when(core != ylo)
        def _():
            s1copy(a, 0).start()

        @pl.when(core == ylo)
        def _():
            s1[a, pl.ds(lax.rem(v, 8), 1)] = ins[a][...][None]

    mate_cols = pl.ds(pl.multiple_of((1 - core) * HALF, 128), HALF)

    def s1_finish(a):
        @pl.loop(0, 8)
        def _(j):
            @pl.when(core * 8 + j != v)
            def _():
                rcopy(ins[a], s1.at[a, j], s1s.at[a, 0], s1r.at[a, j], p, mate).wait_recv()

        block = jnp.concatenate([s1[a, k] for k in range(8)], axis=-1)
        for c in range(2):
            @pl.when(core == c)
            def _():
                bufs[a][yh, zz, :, c * HALF : (c + 1) * HALF] = block

    def s1_drain(a):
        @pl.loop(1, 8)
        def _(i):
            s1copy(a, i).wait_send()

        @pl.when(core != ylo)
        def _():
            s1copy(a, 0).wait_send()

    s1_begin(0)

    def piece(ref, y, z, x):
        return ref.at[
            y, z, pl.ds(pl.multiple_of(lax.rem(x, 2) * 16, 16), 16), pl.ds(pl.multiple_of(x // 2 * QUART, 128), QUART)
        ]

    def part(ref, c, y, z, m):
        return piece(ref, y, z, xx) if c == 0 else ref.at[y, z, :, pl.ds(HALF + m * QUART, QUART)]

    def ycopy(c, a, m):
        b = part(bufs[a], c, yh, zz, m)
        return rcopy(b, b, ys.at[a, m], yr.at[a, m], other_y, v)

    def zcopy(c, a, d, s, k, m):
        y = yh if k == 0 else 1 - yh
        z = lax.rem(zz - s + 8, 8) if d == 0 else lax.rem(zz + s, 8)
        b = part(bufs[a], c, y, z, m)
        return rcopy(b, b, zs.at[a, d, s, k, m], zr.at[a, d, s, k, m], zup if d == 0 else zdn, v)

    def mcopy(c, a, y, z):
        b = bufs[a].at[y, z, :, pl.ds(c * HALF, HALF)]
        return rcopy(b, b, cs.at[a, y, z], cr.at[a, y, z], p, mate)

    def xcopy(a, d, hop, y, z):
        b = piece(bufs[a], y, z, xx if hop == 0 else x_at(3 if d == 0 else 1))
        return rcopy(b, b, xs.at[a, d, hop, y, z], xr.at[a, d, hop, y, z], p, x_dev(1 if d == 0 else 3))

    def has(d, s, k):
        return s < 3 or k == d

    events = [None] + [(s, k, d) for s in range(4) for k in range(2) for d in range(2) if has(d, s, k)]

    def where(e):
        if e is None:
            return 1, 1 - yh, zz
        s, k, d = e
        z = lax.rem(zz - s - 1 + 8, 8) if d == 0 else lax.rem(zz + s + 1, 8)
        return k, (yh if k == 0 else 1 - yh), z

    def on_core(c):
        return pl.when(core == c)

    def ring_begin(a):
        for c in range(2):
            @on_core(c)
            def _():
                for m in range(1 + c):
                    ycopy(c, a, m).start()
                    for d in range(2):
                        zcopy(c, a, d, 0, 0, m).start()
                mcopy(c, a, yh, zz).start()

    def take(c, a, e):
        k, y, z = where(e)
        if e is None:
            for m in range(1 + c):
                ycopy(c, a, m).wait_recv()
                for d in range(2):
                    zcopy(c, a, d, 0, 1, m).start()
        else:
            s, k, d = e
            for m in range(1 + c):
                zcopy(c, a, d, s, k, m).wait_recv()
                if s < 3 and has(d, s + 1, k):
                    zcopy(c, a, d, s + 1, k, m).start()
        if c == 1:
            mcopy(c, a, y, z).start()
        else:
            for d in range(2):
                xcopy(a, d, 0, y, z).start()

    def ring_slots(a, lo, hi):
        @on_core(0)
        def _():
            for i in range(lo, hi):
                if i < 15:
                    take(0, a, events[i])
                if LAG <= i < 15 + LAG:
                    k, y, z = where(events[i - LAG])
                    for d in range(2):
                        xcopy(a, d, 0, y, z).wait_recv()
                    xcopy(a, k, 1, y, z).start()
                if i >= 2 * LAG:
                    k, y, z = where(events[i - 2 * LAG])
                    xcopy(a, k, 1, y, z).wait_recv()
                    mcopy(0, a, y, z).start()

        @on_core(1)
        def _():
            for i in range(min(lo, 15), min(hi, 15)):
                take(1, a, events[i])

    def ring_finish(a):
        for c in range(2):
            @on_core(c)
            def _():
                mcopy(1 - c, a, yh, zz).wait_recv()
                for e in events:
                    _, y, z = where(e)
                    mcopy(1 - c, a, y, z).wait_recv()

    def ring_drain(a):
        for c in range(2):
            @on_core(c)
            def _():
                for m in range(1 + c):
                    ycopy(c, a, m).wait_send()
                mcopy(c, a, yh, zz).wait_send()
                for e in events:
                    k, y, z = where(e)
                    mcopy(c, a, y, z).wait_send()
                    if c == 0:
                        for d in range(2):
                            xcopy(a, d, 0, y, z).wait_send()
                        xcopy(a, k, 1, y, z).wait_send()
                    if e is not None:
                        s, k, d = e
                        for m in range(1 + c):
                            zcopy(c, a, d, s, k, m).wait_send()

        s1_drain(a)

    s1_finish(0)
    ring_begin(0)
    s1_begin(1)
    ring_slots(0, 0, 9)
    s1_finish(1)
    ring_slots(0, 9, SLOTS)
    ring_begin(1)
    ring_finish(0)
    wcopy.wait()

    base = (p * 16 + v) * ROWS
    tgt = tgt_ref[...]

    def row_ids(i, rows):
        return base + i * rows + lax.broadcasted_iota(jnp.int32, (rows, TOKENS), 0)

    sums[...] = jnp.zeros_like(sums)

    for i in range(5):
        r = slice(i * 128, (i + 1) * 128)
        logits = lax.dot_general(w[r, :], h_buf[...].reshape(TOKENS, D), NT, preferred_element_type=F32)
        t = jnp.tanh(logits / 30.0)
        tanh_buf[r, :] = t
        capped = 30.0 * t
        sums[0:1, :] += jnp.sum(jnp.exp(capped), axis=0, keepdims=True)
        sums[1:2, :] += jnp.sum(jnp.where(row_ids(i, 128) == tgt, capped, 0.0), axis=0, keepdims=True)
        ring_slots(1, i, i + 1)

    for k in range(4):
        for r in range(2):
            ar_src[4 * r + k : 4 * r + k + 1, :] = sums[r : r + 1, 128 * k : 128 * k + 128]

    def avcopy(i):
        return rcopy(ar_src, ar_v.at[v], avs.at[i], avr.at[i], p, lax.rem(v + i, 16))

    def apcopy(i):
        return rcopy(ar_src, ar_p.at[p], aps.at[i], apr.at[i], lax.rem(p + i, 16), v)

    @pl.loop(1, 16)
    def _(i):
        avcopy(i).start()
    ar_v[pl.ds(v, 1)] = ar_src[...][None]
    ring_slots(1, 5, 9)

    @pl.loop(1, 16)
    def _(i):
        avcopy(i).wait()
    ar_src[...] = jnp.sum(ar_v[...], axis=0)

    @pl.loop(1, 16)
    def _(i):
        apcopy(i).start()
    ar_p[pl.ds(p, 1)] = ar_src[...][None]
    ring_slots(1, 9, 13)

    @pl.loop(1, 16)
    def _(i):
        apcopy(i).wait()
    whole = jnp.sum(ar_p[...], axis=0)
    sum_exp = jnp.concatenate([whole[k : k + 1] for k in range(4)], axis=-1)
    losses = jnp.log(whole[0:4]) - whole[4:8]
    row = jnp.zeros((1, 128), F32)
    for k in range(4):
        row += jnp.where(p // 4 == k, losses[k : k + 1], 0.0)
    held = jnp.zeros((1, 32), F32)
    for k in range(4):
        held += jnp.where(lax.rem(p, 4) == k, row[:, 32 * k : 32 * k + 32], 0.0)
    loss_out[...] = held

    @pl.loop(0, 5)
    def _(i):
        r = pl.ds(pl.multiple_of(i * 128, 128), 128)
        t = tanh_buf[r, :]
        hit = (row_ids(i, 128) == tgt).astype(F32)
        d = (jnp.exp(30.0 * t) / sum_exp - hit) * (1.0 - t * t)
        dlt[r, :] = d.astype(BF)
        dl[:, r] = d.T.astype(BF)

    ring_slots(1, 13, 15)

    def products(half):
        @pl.loop(0, 3)
        def _(i):
            n = pl.ds(pl.multiple_of(half * HALF + i * 768, 128), 768)
            g = jnp.dot(dl[...], w[:, n], preferred_element_type=F32)
            g_buf[:, :, :, n] = g.astype(BF).reshape(2, 8, 32, 768)

    def pcopy(j):
        z = lax.rem(zz + j, 8)
        return rcopy(g_buf.at[:, z, :, mate_cols], pair.at[:, z], ps.at[j], pr.at[j], p, mate)

    order = (4, 3, 5, 2, 6, 1, 7, 0)
    products(1 - core)
    for j in order:
        pcopy(j).start()
    ring_slots(1, 15, 18)
    products(core)
    ring_slots(1, 18, 20)

    def paired(y, z, c):
        return g_buf[y, z, :, pl.ds(c * HALF, HALF)].astype(F32) + pair[y, z].astype(F32)

    def paired1(y, j, m):
        z = lax.rem(zz + j, 8)
        n = pl.ds(m * QUART, QUART)
        return g_buf[y, z, :, pl.ds(HALF + m * QUART, QUART)].astype(F32) + pair[y, z, :, n].astype(F32)

    def rdest(d, s):
        return lax.rem(zz + 4 - s, 8) if d == 0 else lax.rem(zz + 4 + s, 8)

    def jdest(d, s):
        return 4 - s if d == 0 else lax.rem(4 + s, 8)

    def rpart(ref, c, *at):
        return ref.at[(*at, pl.ds(0, 16), pl.ds(0, QUART))] if c == 0 else ref.at[at]

    def rsrc(c, y, z, m):
        return piece(pair, y, z, xx) if c == 0 else pair.at[y, z, :, pl.ds(m * QUART, QUART)]

    def rdst(c, d, s, y, m):
        return rbuf.at[d, s, y, pl.ds(0, 32 if c else 16), pl.ds(m * QUART, QUART)]

    def rsend(c, d, s, y, m):
        src = rsrc(c, y, rdest(d, s), m)
        return rcopy(src, rdst(c, d, s, y, m), rs.at[d, s, y, m], rr.at[d, s, y, m], zup if d == 0 else zdn, v)

    def rhas(d, s, y):
        return s > 0 or y == d

    def rstep(c, d, s, total_of):
        for y in range(2):
            if rhas(d, s, y):
                z = rdest(d, s)
                for m in range(1 + c):
                    total = total_of(y, jdest(d, s), m)
                    if s > 0 and rhas(d, s - 1, y):
                        rsend(c, d, s - 1, y, m).wait_recv()
                        total += rdst(c, d, s - 1, y, m)[...].astype(F32)
                    rsrc(c, y, z, m)[...] = total.astype(BF)
                    rsend(c, d, s, y, m).start()

    def zof(j):
        return lax.rem(zz + j, 8)

    def x1copy(y, j):
        z = zof(j)
        return rcopy(piece(pair, y, z, x_at(2)), xr1.at[y, z], x1s.at[y, z], x1r.at[y, z], p, x_dev(1 if y == 0 else 3))

    def x2copy(d, y, j):
        z = zof(j)
        to = 1 if d == 0 else 3
        return rcopy(piece(pair, y, z, x_at(to)), xr2.at[d, y, z], x2s.at[d, y, z], x2r.at[d, y, z], p, x_dev(to))

    def xtotal(y, j, m=0):
        z = zof(j)
        return piece(pair, y, z, xx)[...].astype(F32) + xr2[0, y, z].astype(F32) + xr2[1, y, z].astype(F32)

    blocks = [(y, j) for j in order for y in range(2)]
    zsteps = {4: [(0, 0), (1, 0)], 3: [(0, 1)], 5: [(1, 1)], 2: [(0, 2)], 6: [(1, 2)], 1: [(0, 3)], 7: [(1, 3)], 0: []}

    def reduce0(i):
        if i < 16:
            y, j = blocks[i]
            if y == 0:
                pcopy(j).wait_recv()
            pair[y, zof(j)] = paired(y, zof(j), 0).astype(BF)
            x1copy(y, j).start()
        if RLAG <= i < 16 + RLAG:
            y, j = blocks[i - RLAG]
            x1copy(y, j).wait_recv()
            b = piece(pair, y, zof(j), x_at(1 if y == 0 else 3))
            b[...] = (b[...].astype(F32) + xr1[y, zof(j)].astype(F32)).astype(BF)
            for d in range(2):
                x2copy(d, y, j).start()
        if i >= 2 * RLAG:
            y, j = blocks[i - 2 * RLAG]
            for d in range(2):
                x2copy(d, y, j).wait_recv()
            if y == 1:
                for d, s in zsteps[j]:
                    rstep(0, d, s, xtotal)

    def reduce1(i):
        j = order[i]
        pcopy(j).wait_recv()
        for d, s in zsteps[j]:
            rstep(1, d, s, paired1)

    def gcopy(i):
        return pltpu.make_async_copy(g_stage.at[i % 2], grad_out.at[:, i * 512 : (i + 1) * 512], gs.at[i % 2])

    def table(i):
        n = slice(i * 512, (i + 1) * 512)
        sel = (
            base + lax.broadcasted_iota(jnp.int32, (ROWS, TOKENS), 0) == ids_ref[...]
        ).astype(F32).astype(BF)
        acc = jnp.dot(sel, c_buf[:, :, :, n].reshape(TOKENS, 512), preferred_element_type=F32) * (float(D) ** 0.5)
        acc += jnp.dot(dlt[...], h_buf[:, :, :, n].reshape(TOKENS, 512), preferred_element_type=F32)
        if i >= 2:
            gcopy(i - 2).wait()
        g_stage[i % 2] = acc.astype(BF)
        gcopy(i).start()

    for i in range(16 + 2 * RLAG):
        @on_core(0)
        def _():
            reduce0(i)

        if i % 2 == 0 and i < 16:
            @on_core(1)
            def _():
                reduce1(i // 2)

        if i < 5:
            ring_slots(1, 20 + i, 21 + i)
        elif i == 5:
            ring_finish(1)
        if i >= 5 and i % 2 == 1:
            table((i - 5) // 2)

    def last(c, y):
        total = xtotal(y, 0) if c == 0 else paired(y, zz, 1)
        for d in range(2):
            total += rpart(rbuf, c, d, 3, y)[...].astype(F32)
        return total

    def yback(c):
        return rcopy(rpart(y_buf, c, 0), rpart(y_buf, c, 1), yys, yyr, other_y, v)

    def owner(c, k):
        return xx // 2 * 4 + k if c == 0 else 8 + k

    def vcopy(c, k):
        slot = ylo * 2 + lax.rem(xx, 2) if c == 0 else v // 2
        if c == 0:
            return rcopy(v_src.at[k, pl.ds(0, 16)], v_buf.at[slot, pl.ds(0, 16)], vs.at[k], vr.at[slot], p, owner(c, k))
        return rcopy(v_src.at[k], v_buf.at[slot], vs.at[k], vr.at[slot], p, owner(c, k))

    for c in range(2):
        @on_core(c)
        def _():
            for d in range(2):
                for y in range(2):
                    for m in range(1 + c):
                        rsend(c, d, 3, y, m).wait_recv()
            rpart(y_buf, c, 0)[...] = last(c, 1 - yh).astype(BF)
            yback(c).start()
            mine = last(c, yh)
            yback(c).wait()
            mine += rpart(y_buf, c, 1)[...].astype(F32)
            rows = 16 if c == 0 else 32
            count = 4 if c == 0 else 8
            for k in range(count):
                v_src[k, 0:rows] = mine[:, k * PIECE : (k + 1) * PIECE]
            for k in range(count):
                @pl.when(owner(c, k) != v)
                def _():
                    vcopy(c, k).start()

                @pl.when(owner(c, k) == v)
                def _():
                    slot = ylo * 2 + lax.rem(xx, 2) if c == 0 else v // 2
                    v_buf[pl.ds(slot, 1), 0:rows] = v_src[k, 0:rows][None]

    @pl.when(v < 8)
    def _():
        for j in range(4):
            @pl.when((j // 2) * 8 + (v // 4 * 2 + j % 2) * 2 != v)
            def _():
                b = v_buf.at[j, pl.ds(0, 16)]
                rcopy(v_src.at[0, pl.ds(0, 16)], b, vs.at[0], vr.at[j], p, mate).wait_recv()
        for r in range(2):
            hid_out[16 * r : 16 * r + 16, :] = v_buf[r, 0:16] + v_buf[2 + r, 0:16]

    @pl.when(v >= 8)
    def _():
        for j in range(8):
            @pl.when(2 * j + 1 != v)
            def _():
                rcopy(v_src.at[0], v_buf.at[j], vs.at[0], vr.at[j], p, mate).wait_recv()
        hid_out[...] = jnp.sum(v_buf[...], axis=0)

    gcopy(7).wait()
    gcopy(8).wait()
    for a in range(2):
        ring_drain(a)
    for j in order:
        pcopy(j).wait_send()
    for c in range(2):
        @on_core(c)
        def _():
            for k in range(4 if c == 0 else 8):
                @pl.when(owner(c, k) != v)
                def _():
                    vcopy(c, k).wait_send()
            for s in range(4):
                for d in range(2):
                    for y in range(2):
                        if rhas(d, s, y):
                            for m in range(1 + c):
                                rsend(c, d, s, y, m).wait_send()
            if c == 0:
                for y, j in blocks:
                    x1copy(y, j).wait_send()
                    for d in range(2):
                        x2copy(d, y, j).wait_send()


def local(final_hidden, tied_table, target_ids, input_ids, embed_cot):
    vm = pl.BlockSpec(memory_space=pltpu.VMEM)
    sem = pltpu.SemaphoreType.DMA
    grad, hid, loss = pl.pallas_call(
        kernel,
        out_shape=[
            jax.ShapeDtypeStruct((ROWS, D), BF),
            jax.ShapeDtypeStruct((32, PIECE), F32),
            jax.ShapeDtypeStruct((1, 32), F32),
        ],
        in_specs=[vm, pl.BlockSpec(memory_space=pltpu.HBM), vm, vm, vm],
        out_specs=[pl.BlockSpec(memory_space=pl.ANY), vm, vm],
        scratch_shapes=[
            pltpu.VMEM((ROWS, D), BF),
            pltpu.VMEM((2, 8, 32, D), BF),
            pltpu.VMEM((2, 8, 32, D), BF),
            pltpu.VMEM((ROWS, TOKENS), F32),
            pltpu.VMEM((TOKENS, ROWS), BF),
            pltpu.VMEM((ROWS, TOKENS), BF),
            pltpu.VMEM((2, 8, 32, HALF), BF),
            pltpu.VMEM((2, 4, 2, 32, HALF), BF),
            pltpu.VMEM((2, 8, 32, D), BF),
            pltpu.VMEM((2, 8, 32, PIECE), BF),
            pltpu.VMEM((8, TOKENS), F32),
            pltpu.VMEM((8, 128), F32),
            pltpu.VMEM((16, 8, 128), F32),
            pltpu.VMEM((16, 8, 128), F32),
            pltpu.VMEM((2, 32, HALF), BF),
            pltpu.VMEM((8, 32, PIECE), F32),
            pltpu.VMEM((8, 32, PIECE), F32),
            pltpu.VMEM((2, 8, 16, QUART), BF),
            pltpu.VMEM((2, 2, 8, 16, QUART), BF),
            sem, sem((2, 8)), sem((2, 8)), sem((2, 2)), sem((2, 2)),
            sem((2, 2, 4, 2, 2)), sem((2, 2, 4, 2, 2)), sem((2, 2, 8)), sem((2, 2, 8)),
            sem((16,)), sem((16,)), sem((16,)), sem((16,)),
            sem((8,)), sem((8,)), sem((2, 4, 2, 2)), sem((2, 4, 2, 2)), sem, sem, sem((8,)), sem((8,)),
            sem((2, 2, 2, 2, 8)), sem((2, 2, 2, 2, 8)), sem((2, 8)), sem((2, 8)), sem((2, 2, 8)), sem((2, 2, 8)), sem((2,)), pltpu.VMEM((2, ROWS, 512), BF),
        ],
        compiler_params=pltpu.CompilerParams(
            collective_id=0, has_side_effects=True, vmem_limit_bytes=47 << 20
        ),
        name="head_backward",
    )(
        final_hidden,
        tied_table,
        target_ids.reshape(1, TOKENS),
        input_ids.reshape(1, TOKENS),
        embed_cot,
    )
    return (grad, hid, loss.reshape(32))


def solution(mesh):
    placed = (P("pipe", "vocab"), P(("pipe", "vocab"), None), P(), P(), P("pipe", "vocab"))
    return jax.shard_map(
        local,
        mesh=mesh,
        in_specs=placed,
        out_specs=(P(("pipe", "vocab"), None), P("pipe", "vocab"), P("pipe")),
        check_vma=False,
    )
```

```python
import jax
import jax.numpy as jnp
from jax import lax
from jax.experimental import pallas as pl
from jax.experimental.pallas import tpu as pltpu
from jax.sharding import PartitionSpec as P

D = 4608
HALF = D // 2
QUART = D // 4
LAG = 6
RLAG = 4
FIRST = 7
SLOTS = 15 + 2 * LAG
ROWS = 640
TOKENS = 512
PIECE = 288
BF = jnp.bfloat16
F32 = jnp.float32
MESH = pl.DeviceIdType.MESH
NT = (((1,), (1,)), ((), ()))


def rcopy(src, dst, send, recv, p, v):
    return pltpu.make_async_remote_copy(
        src_ref=src, dst_ref=dst, send_sem=send, recv_sem=recv, device_id=(p, v), device_id_type=MESH
    )


def kernel(
    h_in, w_hbm, tgt_ref, ids_ref, c_in,
    grad_out, hid_out, loss_out,
    w, h_buf, c_buf, tanh_buf, dl, dlt, pair, rbuf, g_buf,
    s1, sums, ar_src, ar_v, ar_p, y_buf, v_src, v_buf,
    xr1, xr2,
    w_sem, s1s, s1r, ys, yr, zs, zr, cs, cr, avs, avr, aps, apr, ps, pr, rs, rr, yys, yyr, vs, vr,
    xs, xr, x1s, x1r, x2s, x2r, gs, g_stage,
):
    p = lax.axis_index("pipe")
    v = lax.axis_index("vocab")
    zz = lax.rem(p, 8)
    yh = p // 8
    core = lax.rem(v, 2)
    mate = v + 1 - 2 * core
    xx = lax.rem(v // 2, 4)
    ylo = v // 8
    x_at = lambda i: lax.rem(xx + i, 4)
    x_dev = lambda i: ylo * 8 + x_at(i) * 2 + core
    other_y = lax.rem(p + 8, 16)
    zup = yh * 8 + lax.rem(zz + 1, 8)
    zdn = yh * 8 + lax.rem(zz + 7, 8)
    wcopy = pltpu.make_async_copy(w_hbm, w, w_sem)
    wcopy.start()

    bar = pltpu.get_barrier_semaphore()

    @pl.loop(1, 16)
    def _(i):
        pl.semaphore_signal(bar, inc=1, device_id=(p, lax.rem(v + i, 16)), device_id_type=MESH)

    for q in (other_y, zup, zdn):
        pl.semaphore_signal(bar, inc=1, device_id=(q, v), device_id_type=MESH)
    pl.semaphore_wait(bar, 18)

    bufs = (h_buf, c_buf)
    ins = (h_in, c_in)

    def s1dev(i):
        return lax.rem(v // 2 + i, 8) * 2 + ylo

    def s1copy(a, i):
        return rcopy(ins[a], s1.at[a, lax.rem(v, 8)], s1s.at[a, i], s1r.at[a, lax.rem(v, 8)], p, s1dev(i))

    def s1_begin(a):
        @pl.loop(1, 8)
        def _(i):
            s1copy(a, i).start()

        @pl.when(core != ylo)
        def _():
            s1copy(a, 0).start()

        @pl.when(core == ylo)
        def _():
            s1[a, pl.ds(lax.rem(v, 8), 1)] = ins[a][...][None]

    mate_cols = pl.ds(pl.multiple_of((1 - core) * HALF, 128), HALF)

    def s1_finish(a):
        @pl.loop(0, 8)
        def _(j):
            @pl.when(core * 8 + j != v)
            def _():
                rcopy(ins[a], s1.at[a, j], s1s.at[a, 0], s1r.at[a, j], p, mate).wait_recv()

        block = jnp.concatenate([s1[a, k] for k in range(8)], axis=-1)
        for c in range(2):
            @pl.when(core == c)
            def _():
                bufs[a][yh, zz, :, c * HALF : (c + 1) * HALF] = block

    def s1_drain(a):
        @pl.loop(1, 8)
        def _(i):
            s1copy(a, i).wait_send()

        @pl.when(core != ylo)
        def _():
            s1copy(a, 0).wait_send()

    s1_begin(0)

    def piece(ref, y, z, x):
        return ref.at[
            y, z, pl.ds(pl.multiple_of(lax.rem(x, 2) * 16, 16), 16), pl.ds(pl.multiple_of(x // 2 * QUART, 128), QUART)
        ]

    def part(ref, c, y, z, m):
        return piece(ref, y, z, xx) if c == 0 else ref.at[y, z, :, pl.ds(HALF + m * QUART, QUART)]

    def ycopy(c, a, m):
        b = part(bufs[a], c, yh, zz, m)
        return rcopy(b, b, ys.at[a, m], yr.at[a, m], other_y, v)

    def zcopy(c, a, d, s, k, m):
        y = yh if k == 0 else 1 - yh
        z = lax.rem(zz - s + 8, 8) if d == 0 else lax.rem(zz + s, 8)
        b = part(bufs[a], c, y, z, m)
        return rcopy(b, b, zs.at[a, d, s, k, m], zr.at[a, d, s, k, m], zup if d == 0 else zdn, v)

    def mcopy(c, a, y, z):
        b = bufs[a].at[y, z, :, pl.ds(c * HALF, HALF)]
        return rcopy(b, b, cs.at[a, y, z], cr.at[a, y, z], p, mate)

    def xcopy(a, d, hop, y, z):
        b = piece(bufs[a], y, z, xx if hop == 0 else x_at(3 if d == 0 else 1))
        return rcopy(b, b, xs.at[a, d, hop, y, z], xr.at[a, d, hop, y, z], p, x_dev(1 if d == 0 else 3))

    def has(d, s, k):
        return s < 3 or k == d

    events = [None] + [(s, k, d) for s in range(4) for k in range(2) for d in range(2) if has(d, s, k)]

    def where(e):
        if e is None:
            return 1, 1 - yh, zz
        s, k, d = e
        z = lax.rem(zz - s - 1 + 8, 8) if d == 0 else lax.rem(zz + s + 1, 8)
        return k, (yh if k == 0 else 1 - yh), z

    def on_core(c):
        return pl.when(core == c)

    def ring_begin(a):
        for c in range(2):
            @on_core(c)
            def _():
                for m in range(1 + c):
                    ycopy(c, a, m).start()
                    for d in range(2):
                        zcopy(c, a, d, 0, 0, m).start()
                mcopy(c, a, yh, zz).start()

    def take(c, a, e):
        k, y, z = where(e)
        if e is None:
            for m in range(1 + c):
                ycopy(c, a, m).wait_recv()
                for d in range(2):
                    zcopy(c, a, d, 0, 1, m).start()
        else:
            s, k, d = e
            for m in range(1 + c):
                zcopy(c, a, d, s, k, m).wait_recv()
                if s < 3 and has(d, s + 1, k):
                    zcopy(c, a, d, s + 1, k, m).start()
        if c == 1:
            mcopy(c, a, y, z).start()
        else:
            for d in range(2):
                xcopy(a, d, 0, y, z).start()

    def ring_slots(a, lo, hi):
        @on_core(0)
        def _():
            for i in range(lo, hi):
                if i < 15:
                    take(0, a, events[i])
                if LAG <= i < 15 + LAG:
                    k, y, z = where(events[i - LAG])
                    for d in range(2):
                        xcopy(a, d, 0, y, z).wait_recv()
                    xcopy(a, k, 1, y, z).start()
                if i >= 2 * LAG:
                    k, y, z = where(events[i - 2 * LAG])
                    xcopy(a, k, 1, y, z).wait_recv()
                    mcopy(0, a, y, z).start()

        @on_core(1)
        def _():
            for i in range(min(lo, 15), min(hi, 15)):
                take(1, a, events[i])

    def ring_finish(a):
        for c in range(2):
            @on_core(c)
            def _():
                mcopy(1 - c, a, yh, zz).wait_recv()
                for e in events:
                    _, y, z = where(e)
                    mcopy(1 - c, a, y, z).wait_recv()

    def ring_drain(a):
        for c in range(2):
            @on_core(c)
            def _():
                for m in range(1 + c):
                    ycopy(c, a, m).wait_send()
                mcopy(c, a, yh, zz).wait_send()
                for e in events:
                    k, y, z = where(e)
                    mcopy(c, a, y, z).wait_send()
                    if c == 0:
                        for d in range(2):
                            xcopy(a, d, 0, y, z).wait_send()
                        xcopy(a, k, 1, y, z).wait_send()
                    if e is not None:
                        s, k, d = e
                        for m in range(1 + c):
                            zcopy(c, a, d, s, k, m).wait_send()

        s1_drain(a)

    s1_finish(0)
    ring_begin(0)
    s1_begin(1)
    ring_slots(0, 0, 9)
    s1_finish(1)
    ring_slots(0, 9, SLOTS)
    ring_begin(1)
    ring_finish(0)
    wcopy.wait()

    base = (p * 16 + v) * ROWS
    tgt = tgt_ref[...]

    def row_ids(i, rows):
        return base + i * rows + lax.broadcasted_iota(jnp.int32, (rows, TOKENS), 0)

    sums[...] = jnp.zeros_like(sums)

    for i in range(5):
        r = slice(i * 128, (i + 1) * 128)
        logits = lax.dot_general(w[r, :], h_buf[...].reshape(TOKENS, D), NT, preferred_element_type=F32)
        t = jnp.tanh(logits * (1.0 / 30.0))
        tanh_buf[r, :] = t
        capped = 30.0 * t
        sums[0:1, :] += jnp.sum(jnp.exp(capped), axis=0, keepdims=True)
        sums[1:2, :] += jnp.sum(jnp.where(row_ids(i, 128) == tgt, capped, 0.0), axis=0, keepdims=True)
        ring_slots(1, i, i + 1)

    for k in range(4):
        for r in range(2):
            ar_src[4 * r + k : 4 * r + k + 1, :] = sums[r : r + 1, 128 * k : 128 * k + 128]

    def avcopy(i):
        return rcopy(ar_src, ar_v.at[v], avs.at[i], avr.at[i], p, lax.rem(v + i, 16))

    def apcopy(i):
        return rcopy(ar_src, ar_p.at[p], aps.at[i], apr.at[i], lax.rem(p + i, 16), v)

    @pl.loop(1, 16)
    def _(i):
        avcopy(i).start()
    ar_v[pl.ds(v, 1)] = ar_src[...][None]
    ring_slots(1, 5, 9)

    @pl.loop(1, 16)
    def _(i):
        avcopy(i).wait()
    ar_src[...] = jnp.sum(ar_v[...], axis=0)

    @pl.loop(1, 16)
    def _(i):
        apcopy(i).start()
    ar_p[pl.ds(p, 1)] = ar_src[...][None]
    ring_slots(1, 9, 13)

    @pl.loop(1, 16)
    def _(i):
        apcopy(i).wait()
    whole = jnp.sum(ar_p[...], axis=0)
    sum_exp = jnp.concatenate([whole[k : k + 1] for k in range(4)], axis=-1)
    inverse = 1.0 / sum_exp
    losses = jnp.log(whole[0:4]) - whole[4:8]
    row = jnp.zeros((1, 128), F32)
    for k in range(4):
        row += jnp.where(p // 4 == k, losses[k : k + 1], 0.0)
    held = jnp.zeros((1, 32), F32)
    for k in range(4):
        held += jnp.where(lax.rem(p, 4) == k, row[:, 32 * k : 32 * k + 32], 0.0)
    loss_out[...] = held

    @pl.loop(0, 5)
    def _(i):
        r = pl.ds(pl.multiple_of(i * 128, 128), 128)
        t = tanh_buf[r, :]
        hit = (row_ids(i, 128) == tgt).astype(F32)
        d = (jnp.exp(30.0 * t) * inverse - hit) * (1.0 - t * t)
        dlt[r, :] = d.astype(BF)
        dl[:, r] = d.T.astype(BF)

    ring_slots(1, 13, 15)

    def products(half):
        @pl.loop(0, 3)
        def _(i):
            n = pl.ds(pl.multiple_of(half * HALF + i * 768, 128), 768)
            g = jnp.dot(dl[...], w[:, n], preferred_element_type=F32)
            g_buf[:, :, :, n] = g.astype(BF).reshape(2, 8, 32, 768)

    def pcopy(j):
        z = lax.rem(zz + j, 8)
        return rcopy(g_buf.at[:, z, :, mate_cols], pair.at[:, z], ps.at[j], pr.at[j], p, mate)

    order = (4, 3, 5, 2, 6, 1, 7, 0)
    products(1 - core)
    for j in order:
        pcopy(j).start()
    ring_slots(1, 15, 18)
    products(core)
    ring_slots(1, 18, 20)

    def paired(y, z, c):
        return g_buf[y, z, :, pl.ds(c * HALF, HALF)].astype(F32) + pair[y, z].astype(F32)

    def paired1(y, j, m):
        z = lax.rem(zz + j, 8)
        n = pl.ds(m * QUART, QUART)
        return g_buf[y, z, :, pl.ds(HALF + m * QUART, QUART)].astype(F32) + pair[y, z, :, n].astype(F32)

    def rdest(d, s):
        return lax.rem(zz + 4 - s, 8) if d == 0 else lax.rem(zz + 4 + s, 8)

    def jdest(d, s):
        return 4 - s if d == 0 else lax.rem(4 + s, 8)

    def rpart(ref, c, *at):
        return ref.at[(*at, pl.ds(0, 16), pl.ds(0, QUART))] if c == 0 else ref.at[at]

    def rsrc(c, y, z, m):
        return piece(pair, y, z, xx) if c == 0 else pair.at[y, z, :, pl.ds(m * QUART, QUART)]

    def rdst(c, d, s, y, m):
        return rbuf.at[d, s, y, pl.ds(0, 32 if c else 16), pl.ds(m * QUART, QUART)]

    def rsend(c, d, s, y, m):
        src = rsrc(c, y, rdest(d, s), m)
        return rcopy(src, rdst(c, d, s, y, m), rs.at[d, s, y, m], rr.at[d, s, y, m], zup if d == 0 else zdn, v)

    def rhas(d, s, y):
        return s > 0 or y == d

    def rstep(c, d, s, total_of):
        for y in range(2):
            if rhas(d, s, y):
                z = rdest(d, s)
                for m in range(1 + c):
                    total = total_of(y, jdest(d, s), m)
                    if s > 0 and rhas(d, s - 1, y):
                        rsend(c, d, s - 1, y, m).wait_recv()
                        total += rdst(c, d, s - 1, y, m)[...].astype(F32)
                    rsrc(c, y, z, m)[...] = total.astype(BF)
                    rsend(c, d, s, y, m).start()

    def zof(j):
        return lax.rem(zz + j, 8)

    def x1copy(y, j):
        z = zof(j)
        return rcopy(piece(pair, y, z, x_at(2)), xr1.at[y, z], x1s.at[y, z], x1r.at[y, z], p, x_dev(1 if y == 0 else 3))

    def x2copy(d, y, j):
        z = zof(j)
        to = 1 if d == 0 else 3
        return rcopy(piece(pair, y, z, x_at(to)), xr2.at[d, y, z], x2s.at[d, y, z], x2r.at[d, y, z], p, x_dev(to))

    def xtotal(y, j, m=0):
        z = zof(j)
        return piece(pair, y, z, xx)[...].astype(F32) + xr2[0, y, z].astype(F32) + xr2[1, y, z].astype(F32)

    blocks = [(y, j) for j in order for y in range(2)]
    zsteps = {4: [(0, 0), (1, 0)], 3: [(0, 1)], 5: [(1, 1)], 2: [(0, 2)], 6: [(1, 2)], 1: [(0, 3)], 7: [(1, 3)], 0: []}

    def reduce0(i):
        if i < 16:
            y, j = blocks[i]
            if y == 0:
                pcopy(j).wait_recv()
            pair[y, zof(j)] = paired(y, zof(j), 0).astype(BF)
            x1copy(y, j).start()
        if RLAG <= i < 16 + RLAG:
            y, j = blocks[i - RLAG]
            x1copy(y, j).wait_recv()
            b = piece(pair, y, zof(j), x_at(1 if y == 0 else 3))
            b[...] = (b[...].astype(F32) + xr1[y, zof(j)].astype(F32)).astype(BF)
            for d in range(2):
                x2copy(d, y, j).start()
        if i >= 2 * RLAG:
            y, j = blocks[i - 2 * RLAG]
            for d in range(2):
                x2copy(d, y, j).wait_recv()
            if y == 1:
                for d, s in zsteps[j]:
                    rstep(0, d, s, xtotal)

    def reduce1(i):
        j = order[i]
        pcopy(j).wait_recv()
        for d, s in zsteps[j]:
            rstep(1, d, s, paired1)

    def gcopy(i):
        return pltpu.make_async_copy(g_stage.at[i % 2], grad_out.at[:, i * 512 : (i + 1) * 512], gs.at[i % 2])

    def table(i):
        n = slice(i * 512, (i + 1) * 512)
        sel = (
            base + lax.broadcasted_iota(jnp.int32, (ROWS, TOKENS), 0) == ids_ref[...]
        ).astype(F32).astype(BF)
        acc = jnp.dot(sel, c_buf[:, :, :, n].reshape(TOKENS, 512), preferred_element_type=F32) * (float(D) ** 0.5)
        acc += jnp.dot(dlt[...], h_buf[:, :, :, n].reshape(TOKENS, 512), preferred_element_type=F32)
        if i >= 2:
            gcopy(i - 2).wait()
        g_stage[i % 2] = acc.astype(BF)
        gcopy(i).start()

    for i in range(16 + 2 * RLAG):
        @on_core(0)
        def _():
            reduce0(i)

        if i % 2 == 0 and i < 16:
            @on_core(1)
            def _():
                reduce1(i // 2)

        if i < SLOTS - 20:
            ring_slots(1, 20 + i, 21 + i)
        if i == FIRST:
            ring_finish(1)
        if FIRST <= i < FIRST + 9:
            table(i - FIRST)

    def last(c, y, m):
        for d in range(2):
            rsend(c, d, 3, y, m).wait_recv()
        total = xtotal(y, 0) if c == 0 else paired1(y, 0, m)
        for d in range(2):
            total += rdst(c, d, 3, y, m)[...].astype(F32)
        return total

    def yref(c, i, m):
        return y_buf.at[i, pl.ds(0, 32 if c else 16), pl.ds(m * QUART, QUART)]

    def yback(c, m):
        return rcopy(yref(c, 0, m), yref(c, 1, m), yys.at[m], yyr.at[m], other_y, v)

    def owner(c, k):
        return xx // 2 * 4 + k if c == 0 else 8 + k

    def vcopy(c, k):
        slot = ylo * 2 + lax.rem(xx, 2) if c == 0 else v // 2
        if c == 0:
            return rcopy(v_src.at[k, pl.ds(0, 16)], v_buf.at[slot, pl.ds(0, 16)], vs.at[k], vr.at[slot], p, owner(c, k))
        return rcopy(v_src.at[k], v_buf.at[slot], vs.at[k], vr.at[slot], p, owner(c, k))

    for c in range(2):
        @on_core(c)
        def _():
            rows = 16 if c == 0 else 32
            for m in range(1 + c):
                yref(c, 0, m)[...] = last(c, 1 - yh, m).astype(BF)
                yback(c, m).start()
            for m in range(1 + c):
                mine = last(c, yh, m)
                yback(c, m).wait_recv()
                mine += yref(c, 1, m)[...].astype(F32)
                for i in range(4):
                    v_src[4 * m + i, 0:rows] = mine[:, i * PIECE : (i + 1) * PIECE]
                for k in range(4 * m, 4 * m + 4):
                    @pl.when(owner(c, k) != v)
                    def _():
                        vcopy(c, k).start()

                    @pl.when(owner(c, k) == v)
                    def _():
                        slot = ylo * 2 + lax.rem(xx, 2) if c == 0 else v // 2
                        v_buf[pl.ds(slot, 1), 0:rows] = v_src[k, 0:rows][None]

    @pl.when(v < 8)
    def _():
        for j in range(4):
            @pl.when((j // 2) * 8 + (v // 4 * 2 + j % 2) * 2 != v)
            def _():
                b = v_buf.at[j, pl.ds(0, 16)]
                rcopy(v_src.at[0, pl.ds(0, 16)], b, vs.at[0], vr.at[j], p, mate).wait_recv()
        for r in range(2):
            hid_out[16 * r : 16 * r + 16, :] = v_buf[r, 0:16] + v_buf[2 + r, 0:16]

    @pl.when(v >= 8)
    def _():
        for j in range(8):
            @pl.when(2 * j + 1 != v)
            def _():
                rcopy(v_src.at[0], v_buf.at[j], vs.at[0], vr.at[j], p, mate).wait_recv()
        hid_out[...] = jnp.sum(v_buf[...], axis=0)

    gcopy(7).wait()
    gcopy(8).wait()
    for a in range(2):
        ring_drain(a)
    for j in order:
        pcopy(j).wait_send()
    for c in range(2):
        @on_core(c)
        def _():
            for m in range(1 + c):
                yback(c, m).wait_send()
            for k in range(4 if c == 0 else 8):
                @pl.when(owner(c, k) != v)
                def _():
                    vcopy(c, k).wait_send()
            for s in range(4):
                for d in range(2):
                    for y in range(2):
                        if rhas(d, s, y):
                            for m in range(1 + c):
                                rsend(c, d, s, y, m).wait_send()
            if c == 0:
                for y, j in blocks:
                    x1copy(y, j).wait_send()
                    for d in range(2):
                        x2copy(d, y, j).wait_send()


def local(final_hidden, tied_table, target_ids, input_ids, embed_cot):
    vm = pl.BlockSpec(memory_space=pltpu.VMEM)
    sem = pltpu.SemaphoreType.DMA
    grad, hid, loss = pl.pallas_call(
        kernel,
        out_shape=[
            jax.ShapeDtypeStruct((ROWS, D), BF),
            jax.ShapeDtypeStruct((32, PIECE), F32),
            jax.ShapeDtypeStruct((1, 32), F32),
        ],
        in_specs=[vm, pl.BlockSpec(memory_space=pltpu.HBM), vm, vm, vm],
        out_specs=[pl.BlockSpec(memory_space=pl.ANY), vm, vm],
        scratch_shapes=[
            pltpu.VMEM((ROWS, D), BF),
            pltpu.VMEM((2, 8, 32, D), BF),
            pltpu.VMEM((2, 8, 32, D), BF),
            pltpu.VMEM((ROWS, TOKENS), F32),
            pltpu.VMEM((TOKENS, ROWS), BF),
            pltpu.VMEM((ROWS, TOKENS), BF),
            pltpu.VMEM((2, 8, 32, HALF), BF),
            pltpu.VMEM((2, 4, 2, 32, HALF), BF),
            pltpu.VMEM((2, 8, 32, D), BF),
            pltpu.VMEM((2, 8, 32, PIECE), BF),
            pltpu.VMEM((8, TOKENS), F32),
            pltpu.VMEM((8, 128), F32),
            pltpu.VMEM((16, 8, 128), F32),
            pltpu.VMEM((16, 8, 128), F32),
            pltpu.VMEM((2, 32, HALF), BF),
            pltpu.VMEM((8, 32, PIECE), F32),
            pltpu.VMEM((8, 32, PIECE), F32),
            pltpu.VMEM((2, 8, 16, QUART), BF),
            pltpu.VMEM((2, 2, 8, 16, QUART), BF),
            sem, sem((2, 8)), sem((2, 8)), sem((2, 2)), sem((2, 2)),
            sem((2, 2, 4, 2, 2)), sem((2, 2, 4, 2, 2)), sem((2, 2, 8)), sem((2, 2, 8)),
            sem((16,)), sem((16,)), sem((16,)), sem((16,)),
            sem((8,)), sem((8,)), sem((2, 4, 2, 2)), sem((2, 4, 2, 2)), sem((2,)), sem((2,)), sem((8,)), sem((8,)),
            sem((2, 2, 2, 2, 8)), sem((2, 2, 2, 2, 8)), sem((2, 8)), sem((2, 8)), sem((2, 2, 8)), sem((2, 2, 8)), sem((2,)), pltpu.VMEM((2, ROWS, 512), BF),
        ],
        compiler_params=pltpu.CompilerParams(
            collective_id=0, has_side_effects=True, vmem_limit_bytes=47 << 20
        ),
        name="head_backward",
    )(
        final_hidden,
        tied_table,
        target_ids.reshape(1, TOKENS),
        input_ids.reshape(1, TOKENS),
        embed_cot,
    )
    return (grad, hid, loss.reshape(32))


def solution(mesh):
    placed = (P("pipe", "vocab"), P(("pipe", "vocab"), None), P(), P(), P("pipe", "vocab"))
    return jax.shard_map(
        local,
        mesh=mesh,
        in_specs=placed,
        out_specs=(P(("pipe", "vocab"), None), P("pipe", "vocab"), P("pipe")),
        check_vma=False,
    )
```
